512 devices in a mesh: dp: 32 (over x, z_lo), label: 16 (over y, z_hi, core).
Axes of the slice: x: 4, y: 4, z: 16 (z_hi: 2, z_lo: 8; z = z_hi * 8 + z_lo), core: 2. Of those that a mesh axis runs over, the one named last changes fastest.
Arguments:
- queries: bfloat16 [16384, 1024], P('dp', 'label'), may hold values from -6 to 6
- positives: int32 [16384, 8], P('dp'), may hold values from 0 to 16383, all different within a row
- counts: int32 [16384], P('dp'), may hold values from 1 to 8
- weight: bfloat16 [16384, 1024], P('label'), may hold values from -0.1875 to 0.1875
- master: float32 [16384, 1024], P(('label', 'dp')), may hold values from -0.1875 to 0.1875
- moment_one: float32 [16384, 1024], P(('label', 'dp')), may hold values from -0.024 to 0.024
- moment_two: float32 [16384, 1024], P(('label', 'dp')), may hold values from 1e-08 to 1e-06
Outputs:
- new_weight: bfloat16 [16384, 1024], P('label')
- new_master: float32 [16384, 1024], P(('label', 'dp'))
- new_one: float32 [16384, 1024], P(('label', 'dp'))
- new_two: float32 [16384, 1024], P(('label', 'dp'))
The draws below stay inside these ranges and needn't reach their ends.
Inputs may be any that keep to these rules, and one draw needn't show every extreme that they name: `positives`: the ids in one row are distinct, and every label id appears in some row.
All inputs are finite; a program needn't handle non-finite values.
Results may differ from the reference program's by a relative error of at most 0.0031.
Values may be sent and summed in bfloat16 or wider, within the bound.
No kernel may reach another device: no remote copies, remote signals or barrier semaphores. Data moves between devices by JAX's collectives and lax.ppermute only.
A program may use at most 64 MiB of HBM per device.

```python
import math
import jax
import jax.numpy as jnp
from jax import lax

D = 1024
LAB_DEV = 1024
POS = 8
ADAM_STEP = 10
LABELS = 16384
QUERIES = 16384


def with_ends(entries, key, least, top_value):
    extent = entries.shape
    index_at = [jax.random.randint(jax.random.fold_in(key, axis), (), 0, extent[axis]) for axis in range(len(extent))]
    entries = entries.at[tuple(index_at)].set(least)
    longest = extent.index(max(extent))
    index_at[longest] = (index_at[longest] + 1) % extent[longest]
    return entries.at[tuple(index_at)].set(top_value)


def block_levels(rng, shape, split, low, largest):
    gain, own = 1.0, jax.random.fold_in(rng, 6)
    for dim, blocks in split:
        draws = jnp.exp(jax.random.uniform(jax.random.fold_in(own, dim), (blocks,), jnp.float32, low / len(split), largest / len(split)))
        gain = gain * jnp.repeat(draws, shape[dim] // blocks).reshape([-1 if axis == dim else 1 for axis in range(len(shape))])
    return gain


def choose_distinct(key, rows, count, top, lift):
    sequence = jax.random.permutation(jax.random.fold_in(key, 1), count)
    pull = sequence
    for power in range(3):
        pull = pull * pull // count
    pull = pull * lift // count
    lots = jax.random.randint(jax.random.fold_in(key, 2), (rows, count), 0, 4096) + pull
    fixed_rows = jax.random.permutation(jax.random.fold_in(key, 3), rows)[jnp.arange(count) % rows]
    lots = jnp.where(jnp.arange(rows)[:, None] == fixed_rows[None, :], 1 << 14, lots)
    merit = lots * count + jnp.arange(count)
    return lax.top_k(merit.astype(jnp.int32), top)[1].astype(jnp.int32)


def noise(own_key, extent, scale, bound, pieces=(), held_as=jnp.bfloat16):
    values = jax.random.normal(own_key, extent, jnp.float32) * scale
    if len(pieces) > 0:
        values = block_levels(own_key, extent, pieces, -0.22, 0.18) * values
    return jnp.clip(values, min=-bound, max=bound).astype(held_as)


def setup_inputs(seed: int = 0) -> dict:
    arg_keys = jax.random.split(jax.random.key(seed), 8)
    queries = noise(arg_keys[0], (QUERIES, D), 1.0, 6.0, ((0, 32), (1, 16)))
    positives = choose_distinct(arg_keys[1], QUERIES, LABELS, POS, 4)
    counts = with_ends(jax.random.randint(arg_keys[2], (QUERIES,), 1, POS + 1), jax.random.fold_in(arg_keys[2], 1), 1, POS).astype(jnp.int32)
    weight = noise(arg_keys[3], (LABELS, D), D ** -0.5, 0.1875, ((0, 16),))
    master = noise(arg_keys[4], (LABELS, D), D ** -0.5, 0.1875, ((0, 512),), jnp.float32)
    moment_one = noise(arg_keys[5], (LABELS, D), 0.004, 0.024, ((0, 512),), jnp.float32)
    moment_two = jnp.clip(jnp.exp(math.log(9.999999974752427e-07) - 4.6051702 * jax.random.uniform(arg_keys[6], (LABELS, D), jnp.float32) ** block_levels(arg_keys[6], (LABELS, D), ((0, 512),), -0.2, 0.2)), 9.99999993922529e-09, 9.999999974752427e-07)
    return dict(queries=queries, positives=positives, counts=counts, weight=weight, master=master, moment_one=moment_one, moment_two=moment_two)


def build_target(positives, counts, start, width):
    columns = jnp.arange(width, dtype=jnp.int32)
    shifted = positives - start
    target = jnp.zeros((positives.shape[0], width), jnp.float32)
    for slot in range(positives.shape[1]):
        valid = counts > slot
        match = (shifted[:, slot][:, None] == columns[None, :]) & valid[:, None]
        target = target + match.astype(jnp.float32)
    return target

def reference(queries, positives, counts, weight, master, moment_one, moment_two):
    blocks = weight.reshape(LABELS // LAB_DEV, LAB_DEV, D)
    starts = jnp.arange(LABELS // LAB_DEV, dtype=jnp.int32) * LAB_DEV

    def one_block(pair):
        start, block = pair
        logits = lax.dot_general(queries, block, (((1,), (1,)), ((), ())), preferred_element_type=jnp.float32)
        target = build_target(positives, counts, start, LAB_DEV)
        grad_logit = ((jax.nn.sigmoid(logits) - target) / QUERIES).astype(jnp.bfloat16)
        return lax.dot_general(grad_logit, queries, (((0,), (0,)), ((), ())), preferred_element_type=jnp.float32)
    grad = lax.map(one_block, (starts, blocks)).reshape(LABELS, D)
    new_one = 0.9 * moment_one + 0.1 * grad
    new_two = 0.999 * moment_two + 0.001 * grad * grad
    first = new_one / (1.0 - 0.9 ** ADAM_STEP)
    second = new_two / (1.0 - 0.999 ** ADAM_STEP)
    new_master = master - 0.02 * (first / (jnp.sqrt(second) + 1e-08) + 0.01 * master)
    new_weight = new_master.astype(jnp.bfloat16)
    return (new_weight, new_master, new_one, new_two)
```

```python
import jax
import jax.numpy as jnp
from jax import lax
from jax.experimental import pallas as pl
from jax.experimental.pallas import tpu as pltpu
from jax.sharding import Mesh
from jax.sharding import PartitionSpec as P

ADAM_STEP = 10
AXES = ("x", "zq", "zp", "y", "zh", "c")
DP = ("x", "zq", "zp")
LABEL = ("y", "zh", "c")
SWAP = [(0, 1), (1, 0)]


def grad_kernel(where, own, other, pos_own, pos_other, weight, out, whole, ids):
    core, pair, first_label = where[0], where[1], where[2]
    spans, runs, feats, block = own.shape[0], own.shape[1], own.shape[2], own.shape[3]
    run_count = weight.shape[0]
    run_rows = weight.shape[2]
    rows = run_count * run_rows
    for span in range(spans):
        for run in range(runs):
            at = run * 2 * feats
            whole[span, pl.ds(pl.multiple_of(at + core * feats, feats), feats), :] = own[span, run]
            whole[span, pl.ds(pl.multiple_of(at + (1 - core) * feats, feats), feats), :] = other[span, run]
    ids[pl.ds(pair, 1)] = pos_own[...][None]
    ids[pl.ds(1 - pair, 1)] = pos_other[...][None]
    rows_w = weight[...].reshape(rows, weight.shape[3])
    row = lax.broadcasted_iota(jnp.int32, (rows, 1), 0)
    label = first_label + (row // run_rows) * (2 * run_rows) + row % run_rows
    total = None
    for span in range(spans):
        block_q = whole[span]
        logits = jnp.dot(rows_w, block_q, preferred_element_type=jnp.float32)
        hit = label == ids[span, 0:1, :]
        for slot in range(1, ids.shape[1]):
            hit = hit | (label == ids[span, slot : slot + 1, :])
        diff = jax.nn.sigmoid(logits) - hit.astype(jnp.float32)
        grad_logit = (diff * (1.0 / 16384)).astype(jnp.bfloat16)
        part = lax.dot_general(
            grad_logit, block_q, (((1,), (1,)), ((), ())), preferred_element_type=jnp.float32
        )
        total = part if total is None else total + part
    out[...] = total.astype(jnp.bfloat16)


def summed(terms):
    total = terms[0].astype(jnp.float32)
    for term in range(1, terms.shape[0]):
        total = total + terms[term].astype(jnp.float32)
    return total


def per_device(queries, positives, counts, weight, master, moment_one, moment_two):
    local_q, feats = queries.shape
    labels, width = weight.shape
    own_rows = master.shape[0]
    x_n, zq_n, zp_n = (lax.axis_size(a) for a in DP)
    y_n, zh_n, c_n = (lax.axis_size(a) for a in LABEL)
    core, pair, half = lax.axis_index("c"), lax.axis_index("zp"), lax.axis_index("zh")

    mine = queries.T
    far = lax.ppermute(mine, "zh", SWAP)
    slots = lax.broadcasted_iota(jnp.int32, (positives.shape[1], local_q), 0)
    ids_own = jnp.where(slots < counts[None, :], positives.T, -1)
    ids_other = lax.ppermute(ids_own, "zp", SWAP)

    both = jnp.where(half == 0, jnp.stack([mine, far]), jnp.stack([far, mine]))
    sent = jnp.broadcast_to(both[None], (y_n * zp_n, *both.shape))
    got = lax.all_to_all(sent, ("zp", "y"), 0, 0, tiled=True)
    got = got.reshape(zp_n, y_n * zh_n, feats, local_q)
    got_other = lax.ppermute(got, "c", SWAP)

    runs = weight.reshape(x_n * zq_n, zp_n, own_rows, width)
    rows_w = lax.dynamic_slice_in_dim(runs, pair, 1, 1)
    label_block = lax.axis_index(LABEL)
    first = label_block * labels + pair * own_rows
    where = jnp.stack([core, pair, first]).astype(jnp.int32)
    rows = x_n * zq_n * own_rows
    vmem = pl.BlockSpec(memory_space=pltpu.VMEM)
    part = pl.pallas_call(
        grad_kernel,
        out_shape=jax.ShapeDtypeStruct((rows, width), jnp.bfloat16),
        in_specs=[pl.BlockSpec(memory_space=pltpu.SMEM)] + [vmem] * 5,
        out_specs=vmem,
        scratch_shapes=[
            pltpu.VMEM((zp_n, width, local_q), jnp.bfloat16),
            pltpu.VMEM((zp_n, positives.shape[1], local_q), jnp.int32),
        ],
        cost_estimate=pl.CostEstimate(
            flops=4 * rows * width * zp_n * local_q, bytes_accessed=6 << 20, transcendentals=0
        ),
    )(where, got, got_other, ids_own, ids_other, rows_w)

    by_x = lax.all_to_all(part.reshape(x_n, zq_n * own_rows, width), "x", 0, 0, tiled=True)
    by_x = summed(by_x).astype(jnp.bfloat16)
    by_z = lax.all_to_all(by_x.reshape(zq_n, own_rows, width), "zq", 0, 0, tiled=True)
    grad = summed(by_z)

    new_one = 0.9 * moment_one + 0.1 * grad
    new_two = 0.999 * moment_two + 0.001 * grad * grad
    first = new_one / (1.0 - 0.9**ADAM_STEP)
    second = new_two / (1.0 - 0.999**ADAM_STEP)
    new_master = master - 0.02 * (first / (jnp.sqrt(second) + 1e-08) + 0.01 * master)
    low = new_master.astype(jnp.bfloat16)

    along_z = lax.all_to_all(
        jnp.broadcast_to(low[None], (zq_n, own_rows, width)), "zq", 0, 0, tiled=True
    )
    everywhere = lax.all_to_all(
        jnp.broadcast_to(along_z[None], (x_n * zp_n, zq_n, own_rows, width)),
        ("x", "zp"), 0, 0, tiled=True,
    )
    everywhere = everywhere.reshape(x_n, zp_n, zq_n, own_rows, width)
    new_weight = everywhere.transpose(0, 2, 1, 3, 4).reshape(labels, width)
    return (new_weight, new_master, new_one, new_two)


def solution(mesh):
    torus = Mesh(mesh.devices.reshape(4, 4, 2, 4, 2, 2), AXES)
    in_specs = (
        P(DP, LABEL),
        P(DP, None),
        P(DP),
        P(LABEL, None),
        P(LABEL + DP, None),
        P(LABEL + DP, None),
        P(LABEL + DP, None),
    )
    out_specs = (P(LABEL, None),) + (P(LABEL + DP, None),) * 3
    return jax.shard_map(
        per_device, mesh=torus, in_specs=in_specs, out_specs=out_specs, check_vma=False
    )
```

```python
import jax
import jax.numpy as jnp
from jax import lax
from jax.experimental import pallas as pl
from jax.experimental.pallas import tpu as pltpu
from jax.sharding import Mesh
from jax.sharding import PartitionSpec as P

ADAM_STEP = 10
AXES = ("x", "zf", "zm", "zp", "y", "zh", "c")
DP = ("x", "zf", "zm", "zp")
LABEL = ("y", "zh", "c")
SWAP = [(0, 1), (1, 0)]


def grad_kernel(where, own, other, ids_own, ids_far, weight, out, whole, ids):
    core, far, first_label = where[0], where[1], where[2]
    ys, blocks, halves, feats = own.shape[:4]
    runs, _, run_rows, width = weight.shape
    rows = runs * run_rows
    for y in range(ys):
        for block in range(blocks):
            for half in range(halves):
                at = (y * halves + half) * 2 * feats
                mine = pl.ds(pl.multiple_of(at + core * feats, feats), feats)
                theirs = pl.ds(pl.multiple_of(at + (1 - core) * feats, feats), feats)
                whole[block, mine, :] = own[y, block, half]
                whole[block, theirs, :] = other[y, block, half]
    ids[pl.ds(far, 1)] = ids_own[...][None]
    ids[pl.ds(1 - far, 1)] = ids_far[...][None]
    rows_w = weight[...].reshape(rows, width)
    row = lax.broadcasted_iota(jnp.int32, (rows, 1), 0)
    label = first_label + (row // run_rows) * (2 * run_rows) + row % run_rows
    total = None
    for block in range(blocks):
        block_q = whole[block]
        logits = jnp.dot(rows_w, block_q, preferred_element_type=jnp.float32)
        hit = label == ids[block, 0:1, :]
        for slot in range(1, ids.shape[1]):
            hit = hit | (label == ids[block, slot : slot + 1, :])
        diff = jax.nn.sigmoid(logits) - hit.astype(jnp.float32)
        grad_logit = (diff * (1.0 / 16384)).astype(jnp.bfloat16)
        part = lax.dot_general(
            grad_logit, block_q, (((1,), (1,)), ((), ())), preferred_element_type=jnp.float32
        )
        total = part if total is None else total + part
    out[...] = total.astype(jnp.bfloat16)


def summed(terms):
    total = terms[0].astype(jnp.float32)
    for term in range(1, terms.shape[0]):
        total = total + terms[term].astype(jnp.float32)
    return total


def to_all(array, axes):
    count = lax.axis_size(axes)
    return lax.all_to_all(
        jnp.broadcast_to(array[None], (count, *array.shape)), axes, 0, 0, tiled=True
    )


def per_device(queries, positives, counts, weight, master, moment_one, moment_two):
    local_q, feats = queries.shape
    labels, width = weight.shape
    own_rows = master.shape[0]
    x_n, zf_n, zm_n, zp_n = (lax.axis_size(a) for a in DP)
    y_n, zh_n, c_n = (lax.axis_size(a) for a in LABEL)
    core, far = lax.axis_index("c"), lax.axis_index("zf")
    near_rows = zm_n * zp_n * own_rows
    rows = x_n * near_rows

    slots = lax.broadcasted_iota(jnp.int32, (positives.shape[1], local_q), 0)
    ids_own = jnp.where(slots < counts[None, :], positives.T, -1)
    ids_far = lax.ppermute(ids_own, "zf", SWAP)

    along_z = to_all(queries.T, ("zf", "zh"))
    along_y = to_all(along_z.reshape(zf_n, zh_n, feats, local_q), "y")
    other = lax.ppermute(along_y, "c", SWAP)

    runs = weight.reshape(x_n, zf_n, near_rows, width)
    rows_w = lax.dynamic_slice_in_dim(runs, far, 1, 1)
    first = lax.axis_index(LABEL) * labels + far * near_rows
    where = jnp.stack([core, far, first]).astype(jnp.int32)
    vmem = pl.BlockSpec(memory_space=pltpu.VMEM)
    part = pl.pallas_call(
        grad_kernel,
        out_shape=jax.ShapeDtypeStruct((rows, width), jnp.bfloat16),
        in_specs=[pl.BlockSpec(memory_space=pltpu.SMEM)] + [vmem] * 5,
        out_specs=vmem,
        scratch_shapes=[
            pltpu.VMEM((zf_n, width, local_q), jnp.bfloat16),
            pltpu.VMEM((zf_n, positives.shape[1], local_q), jnp.int32),
        ],
        cost_estimate=pl.CostEstimate(
            flops=4 * rows * width * zf_n * local_q, bytes_accessed=6 << 20, transcendentals=0
        ),
    )(where, along_y, other, ids_own, ids_far, rows_w)

    owners = x_n * zm_n * zp_n
    terms = lax.all_to_all(
        part.reshape(owners, own_rows, width), ("x", "zm", "zp"), 0, 0, tiled=True
    )
    grad = summed(terms)

    new_one = 0.9 * moment_one + 0.1 * grad
    new_two = 0.999 * moment_two + 0.001 * grad * grad
    first = new_one / (1.0 - 0.9**ADAM_STEP)
    second = new_two / (1.0 - 0.999**ADAM_STEP)
    new_master = master - 0.02 * (first / (jnp.sqrt(second) + 1e-08) + 0.01 * master)
    low = new_master.astype(jnp.bfloat16)

    every = to_all(to_all(low, ("zf", "zm")), ("x", "zp"))
    every = every.reshape(x_n, zp_n, zf_n * zm_n, own_rows, width)
    new_weight = every.transpose(0, 2, 1, 3, 4).reshape(labels, width)
    return (new_weight, new_master, new_one, new_two)


def solution(mesh):
    torus = Mesh(mesh.devices.reshape(4, 2, 2, 2, 4, 2, 2), AXES)
    in_specs = (
        P(DP, LABEL),
        P(DP, None),
        P(DP),
        P(LABEL, None),
        P(LABEL + DP, None),
        P(LABEL + DP, None),
        P(LABEL + DP, None),
    )
    out_specs = (P(LABEL, None),) + (P(LABEL + DP, None),) * 3
    return jax.shard_map(
        per_device, mesh=torus, in_specs=in_specs, out_specs=out_specs, check_vma=False
    )
```

```python
import jax
import jax.numpy as jnp
from jax import lax
from jax.experimental import pallas as pl
from jax.experimental.pallas import tpu as pltpu
from jax.sharding import Mesh
from jax.sharding import PartitionSpec as P

ADAM_STEP = 10
AXES = ("x", "zf", "zm", "zp", "y", "zh", "c")
DP = ("x", "zf", "zm", "zp")
LABEL = ("y", "zh", "c")
SWAP = [(0, 1), (1, 0)]


def grad_kernel(where, own, other, ids_own, ids_far, weight, out, whole, ids):
    core, far, first_label = where[0], where[1], where[2]
    ys, blocks, halves, feats = own.shape[:4]
    runs, _, run_rows, width = weight.shape
    rows = runs * run_rows
    for y in range(ys):
        for block in range(blocks):
            for half in range(halves):
                at = (y * halves + half) * 2 * feats
                mine = pl.ds(pl.multiple_of(at + core * feats, feats), feats)
                theirs = pl.ds(pl.multiple_of(at + (1 - core) * feats, feats), feats)
                whole[block, mine, :] = own[y, block, half]
                whole[block, theirs, :] = other[y, block, half]
    ids[pl.ds(far, 1)] = ids_own[...][None]
    ids[pl.ds(1 - far, 1)] = ids_far[...][None]
    rows_w = weight[...].reshape(rows, width)
    row = lax.broadcasted_iota(jnp.int32, (rows, 1), 0)
    label = first_label + (row // run_rows) * (2 * run_rows) + row % run_rows
    total = None
    for block in range(blocks):
        block_q = whole[block]
        logits = jnp.dot(rows_w, block_q, preferred_element_type=jnp.float32)
        hit = label == ids[block, 0:1, :]
        for slot in range(1, ids.shape[1]):
            hit = hit | (label == ids[block, slot : slot + 1, :])
        diff = jax.nn.sigmoid(logits) - hit.astype(jnp.float32)
        grad_logit = (diff * (1.0 / 16384)).astype(jnp.bfloat16)
        part = lax.dot_general(
            grad_logit, block_q, (((1,), (1,)), ((), ())), preferred_element_type=jnp.float32
        )
        total = part if total is None else total + part
    out[...] = total.astype(jnp.bfloat16)


def summed(terms):
    total = terms[0].astype(jnp.float32)
    for term in range(1, terms.shape[0]):
        total = total + terms[term].astype(jnp.float32)
    return total


def to_all(array, axes):
    count = lax.axis_size(axes)
    return lax.all_to_all(
        jnp.broadcast_to(array[None], (count, *array.shape)), axes, 0, 0, tiled=True
    )


def per_device(queries, positives, counts, weight, master, moment_one, moment_two):
    local_q, feats = queries.shape
    labels, width = weight.shape
    own_rows = master.shape[0]
    x_n, zf_n, zm_n, zp_n = (lax.axis_size(a) for a in DP)
    y_n, zh_n, c_n = (lax.axis_size(a) for a in LABEL)
    core, far = lax.axis_index("c"), lax.axis_index("zf")
    near_rows = zm_n * zp_n * own_rows
    rows = x_n * near_rows

    slots = lax.broadcasted_iota(jnp.int32, (positives.shape[1], local_q), 0)
    ids_own = jnp.where(slots < counts[None, :], positives.T, -1)
    ids_far = lax.ppermute(ids_own, "zf", SWAP)

    runs = weight.reshape(x_n, zf_n, near_rows, width)
    rows_w = lax.dynamic_slice_in_dim(runs, far, 1, 1)
    first = lax.axis_index(LABEL) * labels + far * near_rows
    where = jnp.stack([core, far, first]).astype(jnp.int32)

    along_z = to_all(queries.T, ("zf", "zh"))
    along_z, ids_own, ids_far, rows_w, where = lax.optimization_barrier(
        (along_z, ids_own, ids_far, rows_w, where)
    )
    along_y = to_all(along_z.reshape(zf_n, zh_n, feats, local_q), "y")
    other = lax.ppermute(along_y, "c", SWAP)

    vmem = pl.BlockSpec(memory_space=pltpu.VMEM)
    part = pl.pallas_call(
        grad_kernel,
        out_shape=jax.ShapeDtypeStruct((rows, width), jnp.bfloat16),
        in_specs=[pl.BlockSpec(memory_space=pltpu.SMEM)] + [vmem] * 5,
        out_specs=vmem,
        scratch_shapes=[
            pltpu.VMEM((zf_n, width, local_q), jnp.bfloat16),
            pltpu.VMEM((zf_n, positives.shape[1], local_q), jnp.int32),
        ],
        cost_estimate=pl.CostEstimate(
            flops=4 * rows * width * zf_n * local_q, bytes_accessed=6 << 20, transcendentals=0
        ),
    )(where, along_y, other, ids_own, ids_far, rows_w)

    by_x = lax.all_to_all(part.reshape(x_n, near_rows, width), "x", 0, 0, tiled=True)
    by_x = summed(by_x).astype(jnp.bfloat16)
    by_z = lax.all_to_all(
        by_x.reshape(zm_n * zp_n, own_rows, width), ("zm", "zp"), 0, 0, tiled=True
    )
    grad = summed(by_z)

    new_one = 0.9 * moment_one + 0.1 * grad
    new_two = 0.999 * moment_two + 0.001 * grad * grad
    first = new_one / (1.0 - 0.9**ADAM_STEP)
    second = new_two / (1.0 - 0.999**ADAM_STEP)
    new_master = master - 0.02 * (first / (jnp.sqrt(second) + 1e-08) + 0.01 * master)
    low = new_master.astype(jnp.bfloat16)

    every = to_all(to_all(low, ("zf", "zm")), ("x", "zp"))
    every = every.reshape(x_n, zp_n, zf_n * zm_n, own_rows, width)
    new_weight = every.transpose(0, 2, 1, 3, 4).reshape(labels, width)
    return (new_weight, new_master, new_one, new_two)


def solution(mesh):
    torus = Mesh(mesh.devices.reshape(4, 2, 2, 2, 4, 2, 2), AXES)
    in_specs = (
        P(DP, LABEL),
        P(DP, None),
        P(DP),
        P(LABEL, None),
        P(LABEL + DP, None),
        P(LABEL + DP, None),
        P(LABEL + DP, None),
    )
    out_specs = (P(LABEL, None),) + (P(LABEL + DP, None),) * 3
    return jax.shard_map(
        per_device, mesh=torus, in_specs=in_specs, out_specs=out_specs, check_vma=False
    )
```

```python
import jax
import jax.numpy as jnp
from jax import lax
from jax.experimental import pallas as pl
from jax.experimental.pallas import tpu as pltpu
from jax.sharding import Mesh
from jax.sharding import PartitionSpec as P

ADAM_STEP = 10
AXES = ("x", "zf", "zm", "zp", "y", "zh", "c")
DP = ("x", "zf", "zm", "zp")
LABEL = ("y", "zh", "c")
SWAP = [(0, 1), (1, 0)]
STAGGER_NS = 10000


def grad_kernel(own, other, ids, weight, out, whole, rows_w, w_sems, own_sems, other_sems):
    core, far = lax.axis_index("c"), lax.axis_index("zf")
    label_block = lax.axis_index("y") * 4 + lax.axis_index("zh") * 2 + core
    ys, blocks, halves, feats = own.shape[:4]
    runs, _, run_rows, width = weight.shape
    rows = runs * run_rows
    fetched = []
    for run in range(runs):
        fetched.append(pltpu.make_async_copy(
            weight.at[run, far], rows_w.at[pl.ds(run * run_rows, run_rows)], w_sems.at[run]))
        fetched[-1].start()
    placed = []
    for block in range(blocks):
        placed.append([])
        for y in range(ys):
            for half in range(halves):
                at = (y * halves + half) * 2 * feats
                for src, sems, which in ((own, own_sems, core), (other, other_sems, 1 - core)):
                    rows_at = pl.ds(pl.multiple_of(at + which * feats, feats), feats)
                    placed[block].append(pltpu.make_async_copy(
                        src.at[y, block, half], whole.at[block, rows_at],
                        sems.at[(block * ys + y) * halves + half]))
                    placed[block][-1].start()
    row = lax.broadcasted_iota(jnp.int32, (rows, 1), 0)
    first_label = label_block * (2 * rows) + far * run_rows
    label = first_label + (row // run_rows) * (2 * run_rows) + row % run_rows
    for copy in fetched:
        copy.wait()
    total = None
    for block in range(blocks):
        high, low = ids[block, 0].astype(jnp.float32), ids[block, 1].astype(jnp.float32)
        slots = (high * 128.0 + low).astype(jnp.int32)
        for copy in placed[block]:
            copy.wait()
        block_q = whole[block]
        logits = jnp.dot(rows_w[...], block_q, preferred_element_type=jnp.float32)
        hit = label == slots[0:1, :]
        for slot in range(1, slots.shape[0]):
            hit = hit | (label == slots[slot : slot + 1, :])
        diff = jax.nn.sigmoid(logits) - hit.astype(jnp.float32)
        grad_logit = (diff * (1.0 / 16384)).astype(jnp.bfloat16)
        part = lax.dot_general(
            grad_logit, block_q, (((1,), (1,)), ((), ())), preferred_element_type=jnp.float32
        )
        total = part if total is None else total + part
    out[...] = total.astype(jnp.bfloat16)
    if STAGGER_NS:
        @pl.when(core == 1)
        def _():
            pl.delay(STAGGER_NS)


def summed(terms):
    total = terms[0].astype(jnp.float32)
    for term in range(1, terms.shape[0]):
        total = total + terms[term].astype(jnp.float32)
    return total


def to_all(array, axes):
    count = lax.axis_size(axes)
    return lax.all_to_all(
        jnp.broadcast_to(array[None], (count, *array.shape)), axes, 0, 0, tiled=True
    )


def per_device(queries, positives, counts, weight, master, moment_one, moment_two):
    local_q, feats = queries.shape
    labels, width = weight.shape
    own_rows = master.shape[0]
    x_n, zf_n, zm_n, zp_n = (lax.axis_size(a) for a in DP)
    y_n, zh_n, c_n = (lax.axis_size(a) for a in LABEL)
    near_rows = zm_n * zp_n * own_rows
    rows = x_n * near_rows

    slots = lax.broadcasted_iota(jnp.int32, (positives.shape[1], local_q), 0)
    ids = jnp.where(slots < counts[None, :], positives.T, -1)
    ids = jnp.where(lax.axis_index("zh") == 0, ids >> 7, ids & 127).astype(jnp.bfloat16)

    along_z = to_all(jnp.concatenate([queries.T, ids]), ("zf", "zh"))
    along_z = along_z.reshape(zf_n, zh_n, feats + ids.shape[0], local_q)
    along_y = to_all(along_z[:, :, :feats], "y")
    other = lax.ppermute(along_y, "c", SWAP)

    vmem = pl.BlockSpec(memory_space=pltpu.VMEM)
    anywhere = pl.BlockSpec(memory_space=pl.ANY)
    pieces = zf_n * y_n * zh_n
    part = pl.pallas_call(
        grad_kernel,
        out_shape=jax.ShapeDtypeStruct((rows, width), jnp.bfloat16),
        in_specs=[anywhere, anywhere, vmem, anywhere],
        out_specs=vmem,
        scratch_shapes=[
            pltpu.VMEM((zf_n, width, local_q), jnp.bfloat16),
            pltpu.VMEM((rows, width), jnp.bfloat16),
            pltpu.SemaphoreType.DMA((x_n,)),
            pltpu.SemaphoreType.DMA((pieces,)),
            pltpu.SemaphoreType.DMA((pieces,)),
        ],
        compiler_params=pltpu.CompilerParams(vmem_limit_bytes=32 << 20),
        cost_estimate=pl.CostEstimate(
            flops=4 * rows * width * zf_n * local_q, bytes_accessed=6 << 20, transcendentals=0
        ),
    )(along_y, other, along_z[:, :, feats:], weight.reshape(x_n, zf_n, near_rows, width))

    by_x = lax.all_to_all(part.reshape(x_n, near_rows, width), "x", 0, 0, tiled=True)
    by_x = summed(by_x).astype(jnp.bfloat16)
    by_z = lax.all_to_all(
        by_x.reshape(zm_n * zp_n, own_rows, width), ("zm", "zp"), 0, 0, tiled=True
    )
    grad = summed(by_z)

    new_one = 0.9 * moment_one + 0.1 * grad
    new_two = 0.999 * moment_two + 0.001 * grad * grad
    first = new_one / (1.0 - 0.9**ADAM_STEP)
    second = new_two / (1.0 - 0.999**ADAM_STEP)
    new_master = master - 0.02 * (first / (jnp.sqrt(second) + 1e-08) + 0.01 * master)
    low = new_master.astype(jnp.bfloat16)

    every = to_all(to_all(low, ("zf", "zm")), ("x", "zp"))
    every = every.reshape(x_n, zp_n, zf_n * zm_n, own_rows, width)
    new_weight = every.transpose(0, 2, 1, 3, 4).reshape(labels, width)
    return (new_weight, new_master, new_one, new_two)


def solution(mesh):
    torus = Mesh(mesh.devices.reshape(4, 2, 2, 2, 4, 2, 2), AXES)
    in_specs = (
        P(DP, LABEL),
        P(DP, None),
        P(DP),
        P(LABEL, None),
        P(LABEL + DP, None),
        P(LABEL + DP, None),
        P(LABEL + DP, None),
    )
    out_specs = (P(LABEL, None),) + (P(LABEL + DP, None),) * 3
    return jax.shard_map(
        per_device, mesh=torus, in_specs=in_specs, out_specs=out_specs, check_vma=False
    )
```

```python
import jax
import jax.numpy as jnp
from jax import lax
from jax.experimental import pallas as pl
from jax.experimental.pallas import tpu as pltpu
from jax.sharding import Mesh
from jax.sharding import PartitionSpec as P

ADAM_STEP = 10
AXES = ("x", "zf", "zm", "zp", "y", "zh", "c")
DP = ("x", "zf", "zm", "zp")
LABEL = ("y", "zh", "c")
SWAP = [(0, 1), (1, 0)]
STAGGER_NS = 8000


def grad_kernel(own, other, ids, weight, out, whole, rows_w, w_sems):
    core, far = lax.axis_index("c"), lax.axis_index("zf")
    label_block = lax.axis_index("y") * 4 + lax.axis_index("zh") * 2 + core
    ys, blocks, halves, feats = own.shape[:4]
    runs, _, run_rows, width = weight.shape
    rows = runs * run_rows
    fetched = []
    for run in range(runs):
        fetched.append(pltpu.make_async_copy(
            weight.at[run, far], rows_w.at[pl.ds(run * run_rows, run_rows)], w_sems.at[run]))
        fetched[-1].start()
    for y in range(ys):
        for block in range(blocks):
            for half in range(halves):
                at = (y * halves + half) * 2 * feats
                mine = pl.ds(pl.multiple_of(at + core * feats, feats), feats)
                theirs = pl.ds(pl.multiple_of(at + (1 - core) * feats, feats), feats)
                whole[block, mine, :] = own[y, block, half]
                whole[block, theirs, :] = other[y, block, half]
    row = lax.broadcasted_iota(jnp.int32, (rows, 1), 0)
    first_label = label_block * (2 * rows) + far * run_rows
    label = first_label + (row // run_rows) * (2 * run_rows) + row % run_rows
    for copy in fetched:
        copy.wait()
    total = None
    for block in range(blocks):
        high, low = ids[block, 0].astype(jnp.float32), ids[block, 1].astype(jnp.float32)
        slots = (high * 128.0 + low).astype(jnp.int32)
        block_q = whole[block]
        logits = jnp.dot(rows_w[...], block_q, preferred_element_type=jnp.float32)
        hit = label == slots[0:1, :]
        for slot in range(1, slots.shape[0]):
            hit = hit | (label == slots[slot : slot + 1, :])
        diff = jax.nn.sigmoid(logits) - hit.astype(jnp.float32)
        grad_logit = (diff * (1.0 / 16384)).astype(jnp.bfloat16)
        part = lax.dot_general(
            grad_logit, block_q, (((1,), (1,)), ((), ())), preferred_element_type=jnp.float32
        )
        total = part if total is None else total + part
    xs, zs, own_rows = out.shape[0], out.shape[1], out.shape[2]
    for x in range(xs):
        for z in range(zs):
            at = (x * zs + z) * own_rows
            out[jnp.where(core == 0, x, z), jnp.where(core == 0, z, x)] = total[
                at : at + own_rows
            ].astype(jnp.bfloat16)
    if STAGGER_NS:
        @pl.when(core == 1)
        def _():
            pl.delay(STAGGER_NS)


def summed(terms):
    total = terms[0].astype(jnp.float32)
    for term in range(1, terms.shape[0]):
        total = total + terms[term].astype(jnp.float32)
    return total


def to_all(array, axes):
    count = lax.axis_size(axes)
    return lax.all_to_all(
        jnp.broadcast_to(array[None], (count, *array.shape)), axes, 0, 0, tiled=True
    )


def per_device(queries, positives, counts, weight, master, moment_one, moment_two):
    local_q, feats = queries.shape
    labels, width = weight.shape
    own_rows = master.shape[0]
    x_n, zf_n, zm_n, zp_n = (lax.axis_size(a) for a in DP)
    y_n, zh_n, c_n = (lax.axis_size(a) for a in LABEL)
    near_rows = zm_n * zp_n * own_rows
    rows = x_n * near_rows

    slots = lax.broadcasted_iota(jnp.int32, (positives.shape[1], local_q), 0)
    ids = jnp.where(slots < counts[None, :], positives.T, -1)
    ids = jnp.where(lax.axis_index("zh") == 0, ids >> 7, ids & 127).astype(jnp.bfloat16)

    along_z = to_all(jnp.concatenate([queries.T, ids]), ("zf", "zh"))
    along_z = along_z.reshape(zf_n, zh_n, feats + ids.shape[0], local_q)
    along_y = to_all(along_z[:, :, :feats], "y")
    other = lax.ppermute(along_y, "c", SWAP)

    vmem = pl.BlockSpec(memory_space=pltpu.VMEM)
    anywhere = pl.BlockSpec(memory_space=pl.ANY)
    zs = zm_n * zp_n
    part = pl.pallas_call(
        grad_kernel,
        out_shape=jax.ShapeDtypeStruct((x_n, zs, own_rows, width), jnp.bfloat16),
        in_specs=[vmem, vmem, vmem, anywhere],
        out_specs=vmem,
        scratch_shapes=[
            pltpu.VMEM((zf_n, width, local_q), jnp.bfloat16),
            pltpu.VMEM((rows, width), jnp.bfloat16),
            pltpu.SemaphoreType.DMA((x_n,)),
        ],
        compiler_params=pltpu.CompilerParams(vmem_limit_bytes=32 << 20),
        cost_estimate=pl.CostEstimate(
            flops=4 * rows * width * zf_n * local_q, bytes_accessed=6 << 20, transcendentals=0
        ),
    )(along_y, other, along_z[:, :, feats:], weight.reshape(x_n, zf_n, near_rows, width))

    def member(x, z, core):
        return (x * zs + z) * c_n + core

    over_x = [[[member(x, z, core) for x in range(x_n)] for z in range(zs)] for core in range(c_n)]
    over_z = [[[member(x, z, core) for z in range(zs)] for x in range(x_n)] for core in range(c_n)]
    axes = ("x", "zm", "zp", "c")
    terms = lax.all_to_all(
        part, axes, 0, 0, axis_index_groups=over_x[0] + over_z[1], tiled=True
    )
    terms = summed(terms).astype(jnp.bfloat16)
    terms = lax.all_to_all(
        terms, axes, 0, 0, axis_index_groups=over_z[0] + over_x[1], tiled=True
    )
    grad = summed(terms)

    new_one = 0.9 * moment_one + 0.1 * grad
    new_two = 0.999 * moment_two + 0.001 * grad * grad
    first = new_one / (1.0 - 0.9**ADAM_STEP)
    second = new_two / (1.0 - 0.999**ADAM_STEP)
    new_master = master - 0.02 * (first / (jnp.sqrt(second) + 1e-08) + 0.01 * master)
    low = new_master.astype(jnp.bfloat16)

    every = to_all(to_all(low, ("zf", "zm")), ("x", "zp"))
    every = every.reshape(x_n, zp_n, zf_n * zm_n, own_rows, width)
    new_weight = every.transpose(0, 2, 1, 3, 4).reshape(labels, width)
    return (new_weight, new_master, new_one, new_two)


def solution(mesh):
    torus = Mesh(mesh.devices.reshape(4, 2, 2, 2, 4, 2, 2), AXES)
    in_specs = (
        P(DP, LABEL),
        P(DP, None),
        P(DP),
        P(LABEL, None),
        P(LABEL + DP, None),
        P(LABEL + DP, None),
        P(LABEL + DP, None),
    )
    out_specs = (P(LABEL, None),) + (P(LABEL + DP, None),) * 3
    return jax.shard_map(
        per_device, mesh=torus, in_specs=in_specs, out_specs=out_specs, check_vma=False
    )
```

```python
import jax
import jax.numpy as jnp
from jax import lax
from jax.experimental import pallas as pl
from jax.experimental.pallas import tpu as pltpu
from jax.sharding import Mesh
from jax.sharding import PartitionSpec as P

ADAM_STEP = 10
AXES = ("x", "zf", "zm", "zp", "y", "zh", "c")
DP = ("x", "zf", "zm", "zp")
LABEL = ("y", "zh", "c")
SWAP = [(0, 1), (1, 0)]
STAGGER_NS = 10000


def grad_kernel(own, other, weight, out, whole, rows_w, w_sems):
    core, near, zh = lax.axis_index("c"), lax.axis_index("zp"), lax.axis_index("zh")
    label_block = lax.axis_index("y") * 4 + zh * 2 + core
    blocks, ys = own.shape[:2]
    slot_count = 8
    feats = (own.shape[2] - slot_count) // 2
    runs, _, run_rows, width = weight.shape
    rows = runs * run_rows
    fetched = []
    for run in range(runs):
        fetched.append(pltpu.make_async_copy(
            weight.at[run, near], rows_w.at[pl.ds(run * run_rows, run_rows)], w_sems.at[run]))
        fetched[-1].start()
    for y in range(ys):
        for block in range(blocks):
            for swap in range(2):
                half = zh if swap == 0 else 1 - zh
                at = y * 4 * feats + half * 2 * feats
                mine = pl.ds(pl.multiple_of(at + core * feats, feats), feats)
                theirs = pl.ds(pl.multiple_of(at + (1 - core) * feats, feats), feats)
                here = slice(swap * feats, (swap + 1) * feats)
                whole[block, mine, :] = own[block, y, here]
                whole[block, theirs, :] = other[block, y, here]
    row = lax.broadcasted_iota(jnp.int32, (rows, 1), 0)
    first_label = label_block * (2 * rows) + near * run_rows
    label = first_label + (row // run_rows) * (2 * run_rows) + row % run_rows
    for copy in fetched:
        copy.wait()
    total = None
    for block in range(blocks):
        high = own[block, 0, 2 * feats :].astype(jnp.float32)
        low = own[block, 1, 2 * feats :].astype(jnp.float32)
        slots = (high * 128.0 + low).astype(jnp.int32)
        block_q = whole[block]
        logits = jnp.dot(rows_w[...], block_q, preferred_element_type=jnp.float32)
        hit = label == slots[0:1, :]
        for slot in range(1, slot_count):
            hit = hit | (label == slots[slot : slot + 1, :])
        diff = jax.nn.sigmoid(logits) - hit.astype(jnp.float32)
        grad_logit = (diff * (1.0 / 16384)).astype(jnp.bfloat16)
        part = lax.dot_general(
            grad_logit, block_q, (((1,), (1,)), ((), ())), preferred_element_type=jnp.float32
        )
        total = part if total is None else total + part
    out[...] = total.astype(jnp.bfloat16)
    if STAGGER_NS:
        @pl.when(core == 1)
        def _():
            pl.delay(STAGGER_NS)


def summed(terms):
    total = terms[0].astype(jnp.float32)
    for term in range(1, terms.shape[0]):
        total = total + terms[term].astype(jnp.float32)
    return total


def to_all(array, axes):
    count = lax.axis_size(axes)
    return lax.all_to_all(
        jnp.broadcast_to(array[None], (count, *array.shape)), axes, 0, 0, tiled=True
    )


def per_device(queries, positives, counts, weight, master, moment_one, moment_two):
    local_q, feats = queries.shape
    labels, width = weight.shape
    own_rows = master.shape[0]
    x_n, zf_n, zm_n, zp_n = (lax.axis_size(a) for a in DP)
    y_n, zh_n, c_n = (lax.axis_size(a) for a in LABEL)
    zq_n = zf_n * zm_n
    rows = x_n * zq_n * own_rows

    mine = queries.T
    far = lax.ppermute(mine, "zh", SWAP)
    slots = lax.broadcasted_iota(jnp.int32, (positives.shape[1], local_q), 0)
    ids = jnp.where(slots < counts[None, :], positives.T, -1)
    ids = jnp.where(lax.axis_index("y") % 2 == 0, ids >> 7, ids & 127).astype(jnp.bfloat16)
    along_y = to_all(jnp.concatenate([mine, far, ids]), ("zp", "y"))
    along_y = along_y.reshape(zp_n, y_n, 2 * feats + ids.shape[0], local_q)
    other = lax.ppermute(along_y, "c", SWAP)

    vmem = pl.BlockSpec(memory_space=pltpu.VMEM)
    anywhere = pl.BlockSpec(memory_space=pl.ANY)
    part = pl.pallas_call(
        grad_kernel,
        out_shape=jax.ShapeDtypeStruct((rows, width), jnp.bfloat16),
        in_specs=[vmem, vmem, anywhere],
        out_specs=vmem,
        scratch_shapes=[
            pltpu.VMEM((zp_n, width, local_q), jnp.bfloat16),
            pltpu.VMEM((rows, width), jnp.bfloat16),
            pltpu.SemaphoreType.DMA((x_n * zq_n,)),
        ],
        compiler_params=pltpu.CompilerParams(vmem_limit_bytes=32 << 20),
        cost_estimate=pl.CostEstimate(
            flops=4 * rows * width * zp_n * local_q, bytes_accessed=6 << 20, transcendentals=0
        ),
    )(along_y, other, weight.reshape(x_n * zq_n, zp_n, own_rows, width))

    by_x = lax.all_to_all(part.reshape(x_n, zq_n * own_rows, width), "x", 0, 0, tiled=True)
    by_x = summed(by_x).astype(jnp.bfloat16)
    by_z = lax.all_to_all(
        by_x.reshape(zq_n, own_rows, width), ("zf", "zm"), 0, 0, tiled=True
    )
    grad = summed(by_z)

    new_one = 0.9 * moment_one + 0.1 * grad
    new_two = 0.999 * moment_two + 0.001 * grad * grad
    first = new_one / (1.0 - 0.9**ADAM_STEP)
    second = new_two / (1.0 - 0.999**ADAM_STEP)
    new_master = master - 0.02 * (first / (jnp.sqrt(second) + 1e-08) + 0.01 * master)
    low = new_master.astype(jnp.bfloat16)

    every = to_all(to_all(low, ("zf", "zm")), ("x", "zp"))
    every = every.reshape(x_n, zp_n, zf_n * zm_n, own_rows, width)
    new_weight = every.transpose(0, 2, 1, 3, 4).reshape(labels, width)
    return (new_weight, new_master, new_one, new_two)


def solution(mesh):
    torus = Mesh(mesh.devices.reshape(4, 2, 2, 2, 4, 2, 2), AXES)
    in_specs = (
        P(DP, LABEL),
        P(DP, None),
        P(DP),
        P(LABEL, None),
        P(LABEL + DP, None),
        P(LABEL + DP, None),
        P(LABEL + DP, None),
    )
    out_specs = (P(LABEL, None),) + (P(LABEL + DP, None),) * 3
    return jax.shard_map(
        per_device, mesh=torus, in_specs=in_specs, out_specs=out_specs, check_vma=False
    )
```

```python
import jax
import jax.numpy as jnp
from jax import lax
from jax.experimental import pallas as pl
from jax.experimental.pallas import tpu as pltpu
from jax.sharding import Mesh
from jax.sharding import PartitionSpec as P

ADAM_STEP = 10
AXES = ("x", "zf", "zm", "zp", "y", "zh", "c")
DP = ("x", "zf", "zm", "zp")
LABEL = ("y", "zh", "c")
SWAP = [(0, 1), (1, 0)]
STAGGER_NS = 10000


def grad_kernel(own, other, weight, out, whole, rows_w):
    core, near, zh = lax.axis_index("c"), lax.axis_index("zp"), lax.axis_index("zh")
    label_block = lax.axis_index("y") * 4 + zh * 2 + core
    blocks, ys = own.shape[:2]
    slot_count = 8
    feats = (own.shape[2] - slot_count) // 2
    runs, _, run_rows, width = weight.shape
    rows = runs * run_rows
    for run in range(runs):
        rows_w[pl.ds(run * run_rows, run_rows), :] = weight[run, near]
    for y in range(ys):
        for block in range(blocks):
            for swap in range(2):
                half = zh if swap == 0 else 1 - zh
                at = y * 4 * feats + half * 2 * feats
                mine = pl.ds(pl.multiple_of(at + core * feats, feats), feats)
                theirs = pl.ds(pl.multiple_of(at + (1 - core) * feats, feats), feats)
                here = slice(swap * feats, (swap + 1) * feats)
                whole[block, mine, :] = own[block, y, here]
                whole[block, theirs, :] = other[block, y, here]
    row = lax.broadcasted_iota(jnp.int32, (rows, 1), 0)
    first_label = label_block * (2 * rows) + near * run_rows
    label = first_label + (row // run_rows) * (2 * run_rows) + row % run_rows
    total = None
    for block in range(blocks):
        high = own[block, 0, 2 * feats :].astype(jnp.float32)
        low = own[block, 1, 2 * feats :].astype(jnp.float32)
        slots = (high * 128.0 + low).astype(jnp.int32)
        block_q = whole[block]
        logits = jnp.dot(rows_w[...], block_q, preferred_element_type=jnp.float32)
        hit = label == slots[0:1, :]
        for slot in range(1, slot_count):
            hit = hit | (label == slots[slot : slot + 1, :])
        diff = jax.nn.sigmoid(logits) - hit.astype(jnp.float32)
        grad_logit = (diff * (1.0 / 16384)).astype(jnp.bfloat16)
        part = lax.dot_general(
            grad_logit, block_q, (((1,), (1,)), ((), ())), preferred_element_type=jnp.float32
        )
        total = part if total is None else total + part
    out[...] = total.astype(jnp.bfloat16)
    if STAGGER_NS:
        @pl.when(core == 1)
        def _():
            pl.delay(STAGGER_NS)


def pack_kernel(mine, far, ids, out):
    feats = mine.shape[0]
    for copy in range(out.shape[0]):
        out[copy, 0:feats] = mine[...]
        out[copy, feats : 2 * feats] = far[...]
        out[copy, 2 * feats :] = ids[...]


def place_kernel(every, out, sems):
    xs, zps, zqs = every.shape[:3]
    copies = []
    for x in range(xs):
        for zp in range(zps):
            for zq in range(zqs):
                copies.append(pltpu.make_async_copy(
                    every.at[x, zp, zq], out.at[x, zq, zp], sems.at[x, zp, zq]))
                copies[-1].start()
    for copy in copies:
        copy.wait()


def summed(terms):
    total = terms[0].astype(jnp.float32)
    for term in range(1, terms.shape[0]):
        total = total + terms[term].astype(jnp.float32)
    return total


def to_all(array, axes):
    count = lax.axis_size(axes)
    return lax.all_to_all(
        jnp.broadcast_to(array[None], (count, *array.shape)), axes, 0, 0, tiled=True
    )


def per_device(queries, positives, counts, weight, master, moment_one, moment_two):
    local_q, feats = queries.shape
    labels, width = weight.shape
    own_rows = master.shape[0]
    x_n, zf_n, zm_n, zp_n = (lax.axis_size(a) for a in DP)
    y_n, zh_n, c_n = (lax.axis_size(a) for a in LABEL)
    zq_n = zf_n * zm_n
    rows = x_n * zq_n * own_rows

    mine = queries.T
    far = lax.ppermute(mine, "zh", SWAP)
    slots = lax.broadcasted_iota(jnp.int32, (positives.shape[1], local_q), 0)
    ids = jnp.where(slots < counts[None, :], positives.T, -1)
    ids = jnp.where(lax.axis_index("y") % 2 == 0, ids >> 7, ids & 127).astype(jnp.bfloat16)
    vmem = pl.BlockSpec(memory_space=pltpu.VMEM)
    piece_rows = 2 * feats + ids.shape[0]
    sent = pl.pallas_call(
        pack_kernel,
        out_shape=jax.ShapeDtypeStruct((zp_n * y_n, piece_rows, local_q), jnp.bfloat16),
        in_specs=[vmem, vmem, vmem],
        out_specs=vmem,
        compiler_params=pltpu.CompilerParams(vmem_limit_bytes=16 << 20),
    )(mine, far, ids)
    along_y = lax.all_to_all(sent, ("zp", "y"), 0, 0, tiled=True)
    along_y = along_y.reshape(zp_n, y_n, piece_rows, local_q)
    other = lax.ppermute(along_y, "c", SWAP)

    part = pl.pallas_call(
        grad_kernel,
        out_shape=jax.ShapeDtypeStruct((rows, width), jnp.bfloat16),
        in_specs=[vmem, vmem, vmem],
        out_specs=vmem,
        scratch_shapes=[
            pltpu.VMEM((zp_n, width, local_q), jnp.bfloat16),
            pltpu.VMEM((rows, width), jnp.bfloat16),
        ],
        compiler_params=pltpu.CompilerParams(vmem_limit_bytes=32 << 20),
        cost_estimate=pl.CostEstimate(
            flops=4 * rows * width * zp_n * local_q, bytes_accessed=6 << 20, transcendentals=0
        ),
    )(along_y, other, weight.reshape(x_n * zq_n, zp_n, own_rows, width))

    by_x = lax.all_to_all(part.reshape(x_n, zq_n * own_rows, width), "x", 0, 0, tiled=True)
    by_x = summed(by_x).astype(jnp.bfloat16)
    by_z = lax.all_to_all(
        by_x.reshape(zq_n, own_rows, width), ("zf", "zm"), 0, 0, tiled=True
    )
    grad = summed(by_z)

    new_one = 0.9 * moment_one + 0.1 * grad
    new_two = 0.999 * moment_two + 0.001 * grad * grad
    first = new_one / (1.0 - 0.9**ADAM_STEP)
    second = new_two / (1.0 - 0.999**ADAM_STEP)
    new_master = master - 0.02 * (first / (jnp.sqrt(second) + 1e-08) + 0.01 * master)
    low = new_master.astype(jnp.bfloat16)

    every = to_all(to_all(low, ("zf", "zm")), ("x", "zp"))
    new_weight = pl.pallas_call(
        place_kernel,
        out_shape=jax.ShapeDtypeStruct((x_n, zq_n, zp_n, own_rows, width), jnp.bfloat16),
        in_specs=[vmem],
        out_specs=pl.BlockSpec(memory_space=pl.ANY),
        scratch_shapes=[pltpu.SemaphoreType.DMA((x_n, zp_n, zq_n))],
        compiler_params=pltpu.CompilerParams(vmem_limit_bytes=16 << 20),
    )(every.reshape(x_n, zp_n, zq_n, own_rows, width)).reshape(labels, width)
    return (new_weight, new_master, new_one, new_two)


def solution(mesh):
    torus = Mesh(mesh.devices.reshape(4, 2, 2, 2, 4, 2, 2), AXES)
    in_specs = (
        P(DP, LABEL),
        P(DP, None),
        P(DP),
        P(LABEL, None),
        P(LABEL + DP, None),
        P(LABEL + DP, None),
        P(LABEL + DP, None),
    )
    out_specs = (P(LABEL, None),) + (P(LABEL + DP, None),) * 3
    return jax.shard_map(
        per_device, mesh=torus, in_specs=in_specs, out_specs=out_specs, check_vma=False
    )
```

```python
import jax
import jax.numpy as jnp
from jax import lax
from jax.experimental import pallas as pl
from jax.experimental.pallas import tpu as pltpu
from jax.sharding import Mesh
from jax.sharding import PartitionSpec as P

ADAM_STEP = 10
AXES = ("x", "zf", "zm", "zp", "y", "zh", "c")
DP = ("x", "zf", "zm", "zp")
LABEL = ("y", "zh", "c")
SWAP = [(0, 1), (1, 0)]
STAGGER_NS = 10000


def grad_kernel(own, other, weight, out, whole, rows_w):
    core, near, zh = lax.axis_index("c"), lax.axis_index("zp"), lax.axis_index("zh")
    label_block = lax.axis_index("y") * 4 + zh * 2 + core
    blocks, ys = own.shape[:2]
    slot_count = 8
    feats = (own.shape[2] - slot_count) // 2
    runs, _, run_rows, width = weight.shape
    rows = runs * run_rows
    for run in range(runs):
        rows_w[pl.ds(run * run_rows, run_rows), :] = weight[run, near]
    for y in range(ys):
        for block in range(blocks):
            for swap in range(2):
                half = zh if swap == 0 else 1 - zh
                at = y * 4 * feats + half * 2 * feats
                mine = pl.ds(pl.multiple_of(at + core * feats, feats), feats)
                theirs = pl.ds(pl.multiple_of(at + (1 - core) * feats, feats), feats)
                here = slice(swap * feats, (swap + 1) * feats)
                whole[block, mine, :] = own[block, y, here]
                whole[block, theirs, :] = other[block, y, here]
    row = lax.broadcasted_iota(jnp.int32, (rows, 1), 0)
    first_label = label_block * (2 * rows) + near * run_rows
    label = first_label + (row // run_rows) * (2 * run_rows) + row % run_rows
    total = None
    for block in range(blocks):
        high = own[block, 0, 2 * feats :].astype(jnp.float32)
        low = own[block, 1, 2 * feats :].astype(jnp.float32)
        slots = (high * 128.0 + low).astype(jnp.int32)
        block_q = whole[block]
        logits = jnp.dot(rows_w[...], block_q, preferred_element_type=jnp.float32)
        hit = label == slots[0:1, :]
        for slot in range(1, slot_count):
            hit = hit | (label == slots[slot : slot + 1, :])
        diff = jax.nn.sigmoid(logits) - hit.astype(jnp.float32)
        grad_logit = (diff * (1.0 / 16384)).astype(jnp.bfloat16)
        part = lax.dot_general(
            grad_logit, block_q, (((1,), (1,)), ((), ())), preferred_element_type=jnp.float32
        )
        total = part if total is None else total + part
    out[...] = total.astype(jnp.bfloat16)
    if STAGGER_NS:
        @pl.when(core == 1)
        def _():
            pl.delay(STAGGER_NS)


def base_kernel(mine, positives, counts, out):
    feats, slot_count = mine.shape[0], positives.shape[0]
    out[0:feats] = mine[...]
    slot = lax.broadcasted_iota(jnp.int32, positives.shape, 0)
    ids = jnp.where(slot < counts[...], positives[...], -1)
    digit = jnp.where(lax.axis_index("y") % 2 == 0, ids >> 7, ids & 127)
    out[feats : feats + slot_count] = digit.astype(jnp.float32).astype(jnp.bfloat16)


def pack_kernel(base, far, out):
    feats = far.shape[0]
    for copy in range(out.shape[0]):
        out[copy, 0:feats] = base[0:feats]
        out[copy, feats : 2 * feats] = far[...]
        out[copy, 2 * feats :] = base[feats:]


def place_kernel(every, out, sems):
    xs, zps, zqs = every.shape[:3]
    copies = []
    for x in range(xs):
        for zp in range(zps):
            for zq in range(zqs):
                copies.append(pltpu.make_async_copy(
                    every.at[x, zp, zq], out.at[x, zq, zp], sems.at[x, zp, zq]))
                copies[-1].start()
    for copy in copies:
        copy.wait()


def summed(terms):
    total = terms[0].astype(jnp.float32)
    for term in range(1, terms.shape[0]):
        total = total + terms[term].astype(jnp.float32)
    return total


def to_all(array, axes):
    count = lax.axis_size(axes)
    return lax.all_to_all(
        jnp.broadcast_to(array[None], (count, *array.shape)), axes, 0, 0, tiled=True
    )


def per_device(queries, positives, counts, weight, master, moment_one, moment_two):
    local_q, feats = queries.shape
    labels, width = weight.shape
    own_rows = master.shape[0]
    x_n, zf_n, zm_n, zp_n = (lax.axis_size(a) for a in DP)
    y_n, zh_n, c_n = (lax.axis_size(a) for a in LABEL)
    zq_n = zf_n * zm_n
    rows = x_n * zq_n * own_rows

    mine = queries.T
    far = lax.ppermute(mine, "zh", SWAP)
    vmem = pl.BlockSpec(memory_space=pltpu.VMEM)
    slot_count = positives.shape[1]
    piece_rows = 2 * feats + slot_count
    base = pl.pallas_call(
        base_kernel,
        out_shape=jax.ShapeDtypeStruct((feats + slot_count, local_q), jnp.bfloat16),
        in_specs=[vmem, vmem, vmem],
        out_specs=vmem,
        compiler_params=pltpu.CompilerParams(vmem_limit_bytes=16 << 20),
    )(mine, positives.T, counts[None, :])
    sent = pl.pallas_call(
        pack_kernel,
        out_shape=jax.ShapeDtypeStruct((zp_n * y_n, piece_rows, local_q), jnp.bfloat16),
        in_specs=[vmem, vmem],
        out_specs=vmem,
        compiler_params=pltpu.CompilerParams(vmem_limit_bytes=16 << 20),
    )(base, far)
    along_y = lax.all_to_all(sent, ("zp", "y"), 0, 0, tiled=True)
    along_y = along_y.reshape(zp_n, y_n, piece_rows, local_q)
    other = lax.ppermute(along_y, "c", SWAP)

    part = pl.pallas_call(
        grad_kernel,
        out_shape=jax.ShapeDtypeStruct((rows, width), jnp.bfloat16),
        in_specs=[vmem, vmem, vmem],
        out_specs=vmem,
        scratch_shapes=[
            pltpu.VMEM((zp_n, width, local_q), jnp.bfloat16),
            pltpu.VMEM((rows, width), jnp.bfloat16),
        ],
        compiler_params=pltpu.CompilerParams(vmem_limit_bytes=32 << 20),
        cost_estimate=pl.CostEstimate(
            flops=4 * rows * width * zp_n * local_q, bytes_accessed=6 << 20, transcendentals=0
        ),
    )(along_y, other, weight.reshape(x_n * zq_n, zp_n, own_rows, width))

    by_x = lax.all_to_all(part.reshape(x_n, zq_n * own_rows, width), "x", 0, 0, tiled=True)
    by_x = summed(by_x).astype(jnp.bfloat16)
    by_z = lax.all_to_all(
        by_x.reshape(zq_n, own_rows, width), ("zf", "zm"), 0, 0, tiled=True
    )
    grad = summed(by_z)

    new_one = 0.9 * moment_one + 0.1 * grad
    new_two = 0.999 * moment_two + 0.001 * grad * grad
    first = new_one / (1.0 - 0.9**ADAM_STEP)
    second = new_two / (1.0 - 0.999**ADAM_STEP)
    new_master = master - 0.02 * (first / (jnp.sqrt(second) + 1e-08) + 0.01 * master)
    low = new_master.astype(jnp.bfloat16)

    every = to_all(to_all(low, ("zf", "zm")), ("x", "zp"))
    new_weight = pl.pallas_call(
        place_kernel,
        out_shape=jax.ShapeDtypeStruct((x_n, zq_n, zp_n, own_rows, width), jnp.bfloat16),
        in_specs=[vmem],
        out_specs=pl.BlockSpec(memory_space=pl.ANY),
        scratch_shapes=[pltpu.SemaphoreType.DMA((x_n, zp_n, zq_n))],
        compiler_params=pltpu.CompilerParams(vmem_limit_bytes=16 << 20),
    )(every.reshape(x_n, zp_n, zq_n, own_rows, width)).reshape(labels, width)
    return (new_weight, new_master, new_one, new_two)


def solution(mesh):
    torus = Mesh(mesh.devices.reshape(4, 2, 2, 2, 4, 2, 2), AXES)
    in_specs = (
        P(DP, LABEL),
        P(DP, None),
        P(DP),
        P(LABEL, None),
        P(LABEL + DP, None),
        P(LABEL + DP, None),
        P(LABEL + DP, None),
    )
    out_specs = (P(LABEL, None),) + (P(LABEL + DP, None),) * 3
    return jax.shard_map(
        per_device, mesh=torus, in_specs=in_specs, out_specs=out_specs, check_vma=False
    )
```

```python
import jax
import jax.numpy as jnp
from jax import lax
from jax.experimental import pallas as pl
from jax.experimental.pallas import tpu as pltpu
from jax.sharding import Mesh
from jax.sharding import PartitionSpec as P

ADAM_STEP = 10
AXES = ("x", "zf", "zm", "zp", "y", "zh", "c")
DP = ("x", "zf", "zm", "zp")
LABEL = ("y", "zh", "c")
SWAP = [(0, 1), (1, 0)]
STAGGER_NS = 8000


def grad_kernel(own, other, weight, out, whole, rows_w):
    core, near, zh = lax.axis_index("c"), lax.axis_index("zp"), lax.axis_index("zh")
    label_block = lax.axis_index("y") * 4 + zh * 2 + core
    blocks, ys = own.shape[:2]
    slot_count = 8
    feats = (own.shape[2] - slot_count) // 2
    runs, _, run_rows, width = weight.shape
    rows = runs * run_rows
    for run in range(runs):
        rows_w[pl.ds(run * run_rows, run_rows), :] = weight[run, near]
    for y in range(ys):
        for block in range(blocks):
            for swap in range(2):
                half = zh if swap == 0 else 1 - zh
                at = y * 4 * feats + half * 2 * feats
                mine = pl.ds(pl.multiple_of(at + core * feats, feats), feats)
                theirs = pl.ds(pl.multiple_of(at + (1 - core) * feats, feats), feats)
                here = slice(swap * feats, (swap + 1) * feats)
                whole[block, mine, :] = own[block, y, here]
                whole[block, theirs, :] = other[block, y, here]
    row = lax.broadcasted_iota(jnp.int32, (rows, 1), 0)
    first_label = label_block * (2 * rows) + near * run_rows
    label = first_label + (row // run_rows) * (2 * run_rows) + row % run_rows
    total = None
    for block in range(blocks):
        high = own[block, 0, 2 * feats :].astype(jnp.float32)
        low = own[block, 1, 2 * feats :].astype(jnp.float32)
        slots = (high * 128.0 + low).astype(jnp.int32)
        block_q = whole[block]
        logits = jnp.dot(rows_w[...], block_q, preferred_element_type=jnp.float32)
        hit = label == slots[0:1, :]
        for slot in range(1, slot_count):
            hit = hit | (label == slots[slot : slot + 1, :])
        diff = jax.nn.sigmoid(logits) - hit.astype(jnp.float32)
        grad_logit = (diff * (1.0 / 16384)).astype(jnp.bfloat16)
        part = lax.dot_general(
            grad_logit, block_q, (((1,), (1,)), ((), ())), preferred_element_type=jnp.float32
        )
        total = part if total is None else total + part
    out[...] = total.astype(jnp.bfloat16)
    if STAGGER_NS:
        @pl.when(core == 1)
        def _():
            pl.delay(STAGGER_NS)


def base_kernel(mine, positives, counts, out):
    feats, slot_count = mine.shape[0], positives.shape[0]
    out[0:feats] = mine[...]
    slot = lax.broadcasted_iota(jnp.int32, positives.shape, 0)
    ids = jnp.where(slot < counts[...], positives[...], -1)
    digit = jnp.where(lax.axis_index("y") % 2 == 0, ids >> 7, ids & 127)
    out[feats : feats + slot_count] = digit.astype(jnp.float32).astype(jnp.bfloat16)


def pack_kernel(base, far, out):
    feats = far.shape[0]
    for copy in range(out.shape[0]):
        out[copy, 0:feats] = base[0:feats]
        out[copy, feats : 2 * feats] = far[...]
        out[copy, 2 * feats :] = base[feats:]


def place_kernel(every, out, sems):
    xs, zps, zqs = every.shape[:3]
    copies = []
    for x in range(xs):
        for zp in range(zps):
            for zq in range(zqs):
                copies.append(pltpu.make_async_copy(
                    every.at[x, zp, zq], out.at[x, zq, zp], sems.at[x, zp, zq]))
                copies[-1].start()
    for copy in copies:
        copy.wait()


def summed(terms):
    total = terms[0].astype(jnp.float32)
    for term in range(1, terms.shape[0]):
        total = total + terms[term].astype(jnp.float32)
    return total


def to_all(array, axes):
    count = lax.axis_size(axes)
    return lax.all_to_all(
        jnp.broadcast_to(array[None], (count, *array.shape)), axes, 0, 0, tiled=True
    )


def per_device(queries, positives, counts, weight, master, moment_one, moment_two):
    local_q, feats = queries.shape
    labels, width = weight.shape
    own_rows = master.shape[0]
    x_n, zf_n, zm_n, zp_n = (lax.axis_size(a) for a in DP)
    y_n, zh_n, c_n = (lax.axis_size(a) for a in LABEL)
    zq_n = zf_n * zm_n
    rows = x_n * zq_n * own_rows

    mine = queries.T
    far = lax.ppermute(mine, "zh", SWAP)
    vmem = pl.BlockSpec(memory_space=pltpu.VMEM)
    slot_count = positives.shape[1]
    piece_rows = 2 * feats + slot_count
    base = pl.pallas_call(
        base_kernel,
        out_shape=jax.ShapeDtypeStruct((feats + slot_count, local_q), jnp.bfloat16),
        in_specs=[vmem, vmem, vmem],
        out_specs=vmem,
        compiler_params=pltpu.CompilerParams(vmem_limit_bytes=16 << 20),
    )(mine, positives.T, counts[None, :])
    sent = pl.pallas_call(
        pack_kernel,
        out_shape=jax.ShapeDtypeStruct((zp_n * y_n, piece_rows, local_q), jnp.bfloat16),
        in_specs=[vmem, vmem],
        out_specs=vmem,
        compiler_params=pltpu.CompilerParams(vmem_limit_bytes=16 << 20),
    )(base, far)
    along_y = lax.all_to_all(sent, ("zp", "y"), 0, 0, tiled=True)
    along_y = along_y.reshape(zp_n, y_n, piece_rows, local_q)
    other = lax.ppermute(along_y, "c", SWAP)

    part = pl.pallas_call(
        grad_kernel,
        out_shape=jax.ShapeDtypeStruct((rows, width), jnp.bfloat16),
        in_specs=[vmem, vmem, vmem],
        out_specs=vmem,
        scratch_shapes=[
            pltpu.VMEM((zp_n, width, local_q), jnp.bfloat16),
            pltpu.VMEM((rows, width), jnp.bfloat16),
        ],
        compiler_params=pltpu.CompilerParams(vmem_limit_bytes=32 << 20),
        cost_estimate=pl.CostEstimate(
            flops=4 * rows * width * zp_n * local_q, bytes_accessed=6 << 20, transcendentals=0
        ),
    )(along_y, other, weight.reshape(x_n * zq_n, zp_n, own_rows, width))

    by_x = lax.all_to_all(part.reshape(x_n, zq_n * own_rows, width), "x", 0, 0, tiled=True)
    by_x = summed(by_x).astype(jnp.bfloat16)
    by_z = lax.all_to_all(
        by_x.reshape(zq_n, own_rows, width), ("zf", "zm"), 0, 0, tiled=True
    )
    grad = summed(by_z)

    new_one = 0.9 * moment_one + 0.1 * grad
    new_two = 0.999 * moment_two + 0.001 * grad * grad
    first = new_one / (1.0 - 0.9**ADAM_STEP)
    second = new_two / (1.0 - 0.999**ADAM_STEP)
    new_master = master - 0.02 * (first / (jnp.sqrt(second) + 1e-08) + 0.01 * master)
    low = new_master.astype(jnp.bfloat16)

    every = to_all(to_all(low, ("zf", "zm")), ("x", "zp"))
    new_weight = pl.pallas_call(
        place_kernel,
        out_shape=jax.ShapeDtypeStruct((x_n, zq_n, zp_n, own_rows, width), jnp.bfloat16),
        in_specs=[vmem],
        out_specs=pl.BlockSpec(memory_space=pl.ANY),
        scratch_shapes=[pltpu.SemaphoreType.DMA((x_n, zp_n, zq_n))],
        compiler_params=pltpu.CompilerParams(vmem_limit_bytes=16 << 20),
    )(every.reshape(x_n, zp_n, zq_n, own_rows, width)).reshape(labels, width)
    return (new_weight, new_master, new_one, new_two)


def solution(mesh):
    torus = Mesh(mesh.devices.reshape(4, 2, 2, 2, 4, 2, 2), AXES)
    in_specs = (
        P(DP, LABEL),
        P(DP, None),
        P(DP),
        P(LABEL, None),
        P(LABEL + DP, None),
        P(LABEL + DP, None),
        P(LABEL + DP, None),
    )
    out_specs = (P(LABEL, None),) + (P(LABEL + DP, None),) * 3
    return jax.shard_map(
        per_device, mesh=torus, in_specs=in_specs, out_specs=out_specs, check_vma=False
    )
```
